32 devices in a mesh: dp: 16 (over z, y, x), mp: 2 (over core).
Axes of the slice: x: 2, y: 2, z: 4, core: 2. Of those that a mesh axis runs over, the one named last changes fastest.
Arguments:
- inputs: bfloat16 [32768, 4096], P('dp', 'mp'), may hold values from -6 to 6
- cotangents: bfloat16 [32768, 4096], P('dp', 'mp'), may hold values from -6 to 6
- loss_token_mask: int32 [32768], P('dp'), may hold values 0 or 1
- adapter_down_weight: bfloat16 [128, 4096], P(None, 'mp'), may hold values from -0.09375 to 0.09375
- adapter_up_weight: bfloat16 [4096, 128], P('mp'), may hold values from -0.5 to 0.5
- width_projection: bfloat16 [2, 4096, 256], P(None, 'mp'), may hold values from -0.09375 to 0.09375
- rank_projection: bfloat16 [2, 128, 16], replicated, may hold values from -0.5 to 0.5
- targets: float32 [64, 8192], P(None, ('dp', 'mp')), may hold values from -500 to 500
Outputs:
- scores: float32 [128, 64], P('dp')
The draws below stay inside these ranges and needn't reach their ends.
All inputs are finite; a program needn't handle non-finite values. No bound on the sum of `loss_token_mask` on one device may be relied on, other than what follows from the above.
Results may differ from the reference program's by a relative error of at most 0.0003.
Values sent between devices are 32-bit elements; how exact they have to be, the bound alone decides.
A program may use at most 64 MiB of HBM per device.

```python
import math
import jax
import jax.numpy as jnp
from jax import lax

MODEL_WIDTH = 4096
ADAPTER_RANK = 128
SEQ = 256
KP = 256
KQ = 16
NT = 64
FEAT = 8192
NCAND = 128
TOKENS = 32768


def draw_targets(key, part):
    first_matrix, second_matrix = jax.random.split(jax.random.fold_in(key, 17), 2)
    column_scale = jnp.exp(jax.random.uniform(second_matrix, (1, FEAT), jnp.float32, 0.0, math.log(10.0)))
    values = jnp.clip(jax.random.normal(first_matrix, (NT, FEAT), jnp.float32), -4.0, 4.0) * column_scale
    return values.astype(jnp.float32)


def touch_ends(values, key, least, high):
    place = [jax.random.randint(jax.random.fold_in(key, axis), (), 0, length) for axis, length in enumerate(values.shape)]
    main_axis = values.shape.index(max(values.shape))
    next_to = place[:main_axis] + [(place[main_axis] + 1) % values.shape[main_axis]] + place[main_axis + 1:]
    return values.at[tuple(place)].set(least).at[tuple(next_to)].set(high)


def block_scale(stream_key, extent, shards, least, top_value):
    gain = 1.0
    for position, parts in shards:
        heights = jax.random.uniform(jax.random.fold_in(jax.random.fold_in(stream_key, 6), position), (parts,), jnp.float32, least / len(shards), top_value / len(shards))
        gain = gain * jnp.repeat(jnp.exp(heights), extent[position] // parts).reshape((-1,) + (1,) * (len(extent) - 1 - position))
    return gain


def bell_draw(stream_key, shape, spread, bound, pieces=(), kind=jnp.bfloat16):
    drawn = spread * jax.random.normal(stream_key, shape, jnp.float32)
    if pieces:
        drawn = drawn * block_scale(stream_key, shape, pieces, -0.22, 0.18)
    return jnp.clip(drawn, -bound, bound).astype(kind)


def setup_inputs(seed: int = 0) -> dict:
    streams_of = jax.random.split(jax.random.key(seed), 9)
    return {
        "inputs": bell_draw(streams_of[0], (TOKENS, MODEL_WIDTH), 1.0, 6.0, ((0, 16), (1, 2))),
        "cotangents": bell_draw(streams_of[1], (TOKENS, MODEL_WIDTH), 1.0, 6.0, ((0, 16), (1, 2))),
        "loss_token_mask": touch_ends((jax.random.randint(streams_of[2], (TOKENS,), 0, 4) < 3).astype(jnp.int32), jax.random.fold_in(streams_of[2], 1), 0, 1),
        "adapter_down_weight": bell_draw(streams_of[3], (ADAPTER_RANK, MODEL_WIDTH), MODEL_WIDTH ** -0.5, 0.09375, ((1, 2),)),
        "adapter_up_weight": bell_draw(streams_of[4], (MODEL_WIDTH, ADAPTER_RANK), ADAPTER_RANK ** -0.5, 0.5, ((0, 2),)),
        "width_projection": bell_draw(streams_of[5], (2, MODEL_WIDTH, KP), MODEL_WIDTH ** -0.5, 0.09375, ((1, 2),)),
        "rank_projection": bell_draw(streams_of[6], (2, ADAPTER_RANK, KQ), ADAPTER_RANK ** -0.5, 0.5),
        "targets": draw_targets(jax.random.fold_in(streams_of[8], 71), 0),
    }


adapter_scale = 4.0
epsilon = 1e-06

def reference(inputs, cotangents, loss_token_mask, adapter_down_weight, adapter_up_weight, width_projection, rank_projection, targets):
    cols_first = rank_projection[0].astype(jnp.float32)
    cols_second = rank_projection[1].astype(jnp.float32)
    down_weight_wide = adapter_down_weight.astype(jnp.float32)
    up_weight_wide = adapter_up_weight.astype(jnp.float32)
    first_projection = width_projection[0].astype(jnp.float32)
    second_projection = width_projection[1].astype(jnp.float32)

    def one_sample(index):
        start = (index * SEQ).astype(jnp.int32)
        layer_activations = lax.dynamic_slice_in_dim(inputs, start, SEQ, 0)
        grads_out = lax.dynamic_slice_in_dim(cotangents, start, SEQ, 0)
        flags = lax.dynamic_slice_in_dim(loss_token_mask, start, SEQ, 0)
        masked_gradient = grads_out * flags.astype(jnp.bfloat16)[:, None]
        wide_activations = layer_activations.astype(jnp.float32)
        wide_masked = masked_gradient.astype(jnp.float32)
        down_rank_product = jnp.dot(wide_activations, down_weight_wide.T, precision=lax.Precision.HIGHEST)
        up_rank_product = jnp.dot(wide_masked, up_weight_wide, precision=lax.Precision.HIGHEST)
        projected_activations = jnp.dot(wide_activations, first_projection, precision=lax.Precision.HIGHEST)
        projected_masked_gradient = jnp.dot(wide_masked, second_projection, precision=lax.Precision.HIGHEST)
        compact_up_gradient = jnp.dot(up_rank_product, cols_first, precision=lax.Precision.HIGHEST)
        compact_down_gradient = jnp.dot(down_rank_product, cols_second, precision=lax.Precision.HIGHEST)
        first_matrix = adapter_scale * jnp.dot(projected_activations.T, compact_up_gradient, precision=lax.Precision.HIGHEST)
        second_matrix = adapter_scale * jnp.dot(projected_masked_gradient.T, compact_down_gradient, precision=lax.Precision.HIGHEST)
        return jnp.concatenate([first_matrix.reshape(-1), second_matrix.reshape(-1)])
    features = lax.map(one_sample, jnp.arange(NCAND, dtype=jnp.int32))
    inner = jnp.dot(features, targets.T, precision=lax.Precision.HIGHEST)
    sample_rms = jnp.sqrt(lax.optimization_barrier(jnp.mean(features * features, axis=1)) + epsilon)
    target_rms = jnp.sqrt(lax.optimization_barrier(jnp.mean(targets * targets, axis=1)) + epsilon)
    return inner / (math.sqrt(FEAT) * sample_rms[:, None] * target_rms[None, :])
```

```python
import functools
import math

import jax
import jax.numpy as jnp
from jax import lax
from jax.experimental import pallas as pl
from jax.experimental.pallas import tpu as pltpu
from jax.sharding import PartitionSpec as P

SEQ = 256
KP = 256
KQ = 16
FEAT = 8192
PLANE = 4
LAG = 2

adapter_scale = 4.0
epsilon = 1e-06

f32 = jnp.float32
bf16 = jnp.bfloat16


def split(value):
    high = value.astype(bf16)
    low = (value - high.astype(f32)).astype(bf16)
    return high, low


def kernel(
    n_dp, samples,
    x_hbm, g_hbm, mask_ref, down_hbm, up_hbm, wp_hbm, rp_ref, tgt_ref, out_ref,
    xv, gv, dv, uv, wv, w2, acol, cs, cr, ys, tp, tt, tth, ttl, fs, fr, es, er,
    xsem, gsem, wsem, zsend, zrecv, psend, csend, crecv, fsend, frecv, esend, erecv,
):
    me = lax.axis_index("dp")
    core = lax.axis_index("mp")
    lines = n_dp // PLANE
    mine_z = lax.div(me, PLANE)
    mine_p = lax.rem(me, PLANE)
    width = xv.shape[2]
    chunk = width // samples
    rows_of = n_dp * KQ

    down_copy = pltpu.make_async_copy(down_hbm, dv, wsem.at[0])
    up_copy = pltpu.make_async_copy(up_hbm, uv, wsem.at[1])
    wp_copy = pltpu.make_async_copy(wp_hbm, wv, wsem.at[2])

    def x_copy(n):
        rows = pl.ds(pl.multiple_of(n * SEQ, SEQ), SEQ)
        return pltpu.make_async_copy(x_hbm.at[rows], xv.at[n], xsem.at[n])

    def g_copy(n):
        rows = pl.ds(pl.multiple_of(n * SEQ, SEQ), SEQ)
        return pltpu.make_async_copy(g_hbm.at[rows], gv.at[n], gsem.at[n])

    down_copy.start()
    up_copy.start()
    for n in range(samples):
        x_copy(n).start()
        g_copy(n).start()
        if n == 0:
            wp_copy.start()

    def z_peer(r):
        return lax.rem(mine_z + r, lines) * PLANE + mine_p

    def p_peer(r):
        return mine_z * PLANE + lax.rem(mine_p + r, PLANE)

    barrier = pltpu.get_barrier_semaphore()
    for r in range(1, lines):
        pl.semaphore_signal(barrier, inc=1, device_id={"dp": z_peer(r)}, device_id_type=pl.DeviceIdType.MESH)
    for r in range(1, PLANE):
        pl.semaphore_signal(barrier, inc=1, device_id={"dp": p_peer(r)}, device_id_type=pl.DeviceIdType.MESH)
    pl.semaphore_signal(barrier, inc=1, device_id={"mp": 1 - core}, device_id_type=pl.DeviceIdType.MESH)

    turned = tgt_ref[...].T
    nt = tgt_ref.shape[0]
    tp[:, 0:nt] = turned
    tp[:, nt : 2 * nt] = turned
    lane = lax.broadcasted_iota(jnp.int32, (KQ, 2 * nt), 1)
    mine_rows = pl.ds(pl.multiple_of(me * KQ, KQ), KQ)
    for pair in range(KQ // 2):
        even = tp[pl.ds(2 * pair, KQ, stride=KQ), :]
        odd = tp[pl.ds(2 * pair + 1, KQ, stride=KQ), :]
        tt[mine_rows, pair * 2 * nt : (pair + 1) * 2 * nt] = jnp.where(lane < nt, even, odd)

    pl.semaphore_wait(barrier, lines - 1 + PLANE - 1 + 1)

    def shard_copy(shard, target, send):
        rows = pl.ds(pl.multiple_of(shard * KQ, KQ), KQ)
        return pltpu.make_async_remote_copy(
            src_ref=tt.at[rows], dst_ref=tt.at[rows], send_sem=send, recv_sem=zrecv.at[shard],
            device_id={"dp": target}, device_id_type=pl.DeviceIdType.MESH,
        )

    for r in range(1, lines):
        shard_copy(me, z_peer(r), zsend.at[r]).start()

    def forward(r):
        for p in range(1, PLANE):
            shard_copy(z_peer(r), p_peer(p), psend.at[r, p]).start()

    def arrived(shard):
        shard_copy(shard, p_peer(1), zsend.at[0]).wait_recv()

    forward(0)

    down_copy.wait()
    up_copy.wait()
    first = lax.dot_general(rp_ref[1], dv[...], (((0,), (0,)), ((), ())), preferred_element_type=f32)
    high, low = split(first)
    acol[0] = jnp.concatenate([high.astype(f32), low.astype(f32)], axis=0).T.astype(bf16)
    second = jnp.dot(uv[...], rp_ref[0], preferred_element_type=f32)
    high, low = split(second)
    acol[1, :, 0:KQ] = high
    acol[1, :, KQ : 2 * KQ] = low

    def c_copy(n):
        return pltpu.make_async_remote_copy(
            src_ref=cs.at[n], dst_ref=cr.at[n], send_sem=csend.at[n], recv_sem=crecv.at[n],
            device_id={"mp": 1 - core}, device_id_type=pl.DeviceIdType.MESH,
        )

    def phase_one(n):
        x_copy(n).wait()
        down = jnp.dot(xv[n], acol[0], preferred_element_type=f32)
        g_copy(n).wait()
        up = jnp.dot(gv[n], acol[1], preferred_element_type=f32)
        down_t = down.T
        up_t = up.T
        cs[n, 0:KQ] = down_t[0:KQ] + down_t[KQ : 2 * KQ]
        cs[n, KQ : 2 * KQ] = up_t[0:KQ] + up_t[KQ : 2 * KQ]
        c_copy(n).start()

    half = samples * KQ

    def phase_two(n):
        c_copy(n).wait_recv()
        flags = mask_ref[n].astype(f32) * adapter_scale
        total = (cs[n] + cr[n]) * flags
        high, low = split(total)
        rows = pl.ds(pl.multiple_of(n * KQ, KQ), KQ)
        low_rows = pl.ds(pl.multiple_of(half + n * KQ, KQ), KQ)
        for j, (data, base) in enumerate(((xv, KQ), (gv, 0))):
            left = jnp.concatenate([high[base : base + KQ], low[base : base + KQ]], axis=0)
            out = jnp.dot(left, data[n], preferred_element_type=f32)
            y_high, y_low = split(out[0:KQ] + out[KQ : 2 * KQ])
            ys[j, rows] = y_high
            ys[j, low_rows] = y_low

    new = lax.broadcasted_iota(jnp.int32, (KP, KP), 1)
    old = lax.broadcasted_iota(jnp.int32, (KP, KP), 0)
    group = KP // 2
    wanted = lax.div(lax.rem(new, group), KQ) * (2 * KQ) + lax.div(new, group) * KQ + lax.rem(new, KQ)
    order = jnp.where(old == wanted, 1.0, 0.0).astype(bf16)

    def reorder(n):
        rows = pl.ds(pl.multiple_of(n * chunk, chunk), chunk)
        for j in range(2):
            w2[j, rows] = jnp.dot(wv[j, rows], order, preferred_element_type=f32).astype(bf16)

    def both(n, carry):
        phase_one(n)
        phase_two(n - LAG)
        return carry

    def only_one(n, carry):
        phase_one(n)
        return carry

    def only_two(n, carry):
        phase_two(n)
        return carry

    def order_step(n, carry):
        reorder(n)
        return carry

    lax.fori_loop(0, LAG, only_one, 0)
    wp_copy.wait()
    lax.fori_loop(0, samples, order_step, 0)
    near = [r for r in range(1, lines)]
    cut = LAG + (samples - LAG) // 2
    lax.fori_loop(LAG, cut, both, 0)
    for r in near:
        arrived(z_peer(r))
        forward(r)
    lax.fori_loop(cut, samples, both, 0)
    lax.fori_loop(samples - LAG, samples, only_two, 0)

    for j in range(2):
        part = jnp.dot(ys[j], w2[j], preferred_element_type=f32)
        part = part[0:half] + part[half : 2 * half]
        for p in range(2):
            fs[p, :, j * group : (j + 1) * group] = part[:, p * group : (p + 1) * group]
    f_copy = pltpu.make_async_remote_copy(
        src_ref=fs.at[1 - core], dst_ref=fr, send_sem=fsend, recv_sem=frecv,
        device_id={"mp": 1 - core}, device_id_type=pl.DeviceIdType.MESH,
    )
    f_copy.start()

    for p in range(1, PLANE):
        for z in range(lines):
            arrived(z * PLANE + lax.rem(mine_p + p, PLANE))

    cols = KQ * nt

    def split_targets(b, carry):
        rows = pl.ds(pl.multiple_of(b * KQ, KQ), KQ)
        block = tt[rows]
        high, low = split(block)
        tth[rows] = high
        ttl[rows] = low
        return carry + block[0:8] * block[0:8] + block[8:16] * block[8:16]

    squares = lax.fori_loop(0, n_dp, split_targets, jnp.zeros((8, cols), f32))
    squares = jnp.sum(squares, axis=0, keepdims=True)

    def fold(value):
        total = value[:, 0 : 2 * nt]
        for piece in range(1, KQ // 2):
            total = total + value[:, piece * 2 * nt : (piece + 1) * 2 * nt]
        return total

    squares = fold(squares)
    es[16:24] = jnp.broadcast_to(squares, (8, 2 * nt))

    f_copy.wait()
    features = fs[core] + fr[...]
    high, low = split(features)
    inner = (
        jnp.dot(high, tth[...], preferred_element_type=f32)
        + jnp.dot(low, tth[...], preferred_element_type=f32)
        + jnp.dot(high, ttl[...], preferred_element_type=f32)
    )
    row_q = lax.rem(lax.broadcasted_iota(jnp.int32, (half, cols), 0), KQ)
    col_q = lax.div(lax.broadcasted_iota(jnp.int32, (half, cols), 1), nt)
    inner = jnp.where(row_q == col_q, inner, 0.0)
    inner = jnp.sum(inner.reshape(samples, KQ, cols), axis=1)
    es[0:8] = fold(inner)
    power = jnp.sum((features * features).reshape(samples, KQ, KP), axis=1)
    es[8:16] = power[:, 0 : KP // 2] + power[:, KP // 2 :]
    e_copy = pltpu.make_async_remote_copy(
        src_ref=es, dst_ref=er, send_sem=esend, recv_sem=erecv,
        device_id={"mp": 1 - core}, device_id_type=pl.DeviceIdType.MESH,
    )
    e_copy.start()
    for r in range(1, lines):
        shard_copy(me, z_peer(r), zsend.at[r]).wait_send()
    for r in range(lines):
        for p in range(1, PLANE):
            shard_copy(z_peer(r), p_peer(p), psend.at[r, p]).wait_send()
    for n in range(samples):
        c_copy(n).wait_send()
    e_copy.wait()
    total = es[...] + er[...]
    sample_rms = jnp.sqrt(jnp.sum(total[8:16], axis=1, keepdims=True) / FEAT + epsilon)
    target_squares = total[16:24, 0:nt] + total[16:24, nt : 2 * nt]
    target_rms = jnp.sqrt(target_squares / FEAT + epsilon)
    product = total[0:8, 0:nt] + total[0:8, nt : 2 * nt]
    out_ref[...] = product / (math.sqrt(FEAT) * sample_rms * target_rms)


def fused(n_dp, inputs, cotangents, loss_token_mask, adapter_down_weight, adapter_up_weight,
          width_projection, rank_projection, targets):
    samples = inputs.shape[0] // SEQ
    width = inputs.shape[1]
    rank = adapter_down_weight.shape[0]
    nt = targets.shape[0]
    any_spec = pl.BlockSpec(memory_space=pl.ANY)
    vmem = pl.BlockSpec(memory_space=pltpu.VMEM)
    dma = pltpu.SemaphoreType.DMA
    lines = n_dp // PLANE
    return pl.pallas_call(
        functools.partial(kernel, n_dp, samples),
        out_shape=jax.ShapeDtypeStruct((samples, nt), f32),
        in_specs=[any_spec, any_spec, vmem, any_spec, any_spec, any_spec, vmem, vmem],
        out_specs=vmem,
        scratch_shapes=[
            pltpu.VMEM((samples, SEQ, width), bf16),
            pltpu.VMEM((samples, SEQ, width), bf16),
            pltpu.VMEM((rank, width), bf16),
            pltpu.VMEM((width, rank), bf16),
            pltpu.VMEM((2, width, KP), bf16),
            pltpu.VMEM((2, width, KP), bf16),
            pltpu.VMEM((2, width, 2 * KQ), bf16),
            pltpu.VMEM((samples, 2 * KQ, SEQ), f32),
            pltpu.VMEM((samples, 2 * KQ, SEQ), f32),
            pltpu.VMEM((2, 2 * samples * KQ, width), bf16),
            pltpu.VMEM((KQ * KQ, 2 * nt), f32),
            pltpu.VMEM((n_dp * KQ, KQ * nt), f32),
            pltpu.VMEM((n_dp * KQ, KQ * nt), bf16),
            pltpu.VMEM((n_dp * KQ, KQ * nt), bf16),
            pltpu.VMEM((2, samples * KQ, KP), f32),
            pltpu.VMEM((samples * KQ, KP), f32),
            pltpu.VMEM((24, 2 * nt), f32),
            pltpu.VMEM((24, 2 * nt), f32),
            dma((samples,)), dma((samples,)), dma((3,)),
            dma((lines,)), dma((n_dp,)), dma((lines, PLANE)),
            dma((samples,)), dma((samples,)), dma, dma, dma, dma,
        ],
        compiler_params=pltpu.CompilerParams(
            collective_id=0, has_side_effects=True, vmem_limit_bytes=56 << 20
        ),
        name="influence",
    )(inputs, cotangents, loss_token_mask.reshape(samples, 1, SEQ), adapter_down_weight,
      adapter_up_weight, width_projection, rank_projection, targets)


def general(inputs, cotangents, loss_token_mask, adapter_down_weight, adapter_up_weight,
            width_projection, rank_projection, targets):
    samples = inputs.shape[0] // SEQ
    masked_gradient = cotangents * loss_token_mask.astype(bf16)[:, None]
    cols_first = rank_projection[0].astype(f32)
    cols_second = rank_projection[1].astype(f32)
    down_partial = jnp.dot(inputs, adapter_down_weight.T, preferred_element_type=f32)
    up_partial = jnp.dot(masked_gradient, adapter_up_weight, preferred_element_type=f32)
    exact = lax.Precision.HIGHEST
    compact_up, compact_down = lax.psum(
        (jnp.dot(up_partial, cols_first, precision=exact), jnp.dot(down_partial, cols_second, precision=exact)), "mp"
    )
    projected_x = jnp.dot(inputs, width_projection[0], preferred_element_type=f32).reshape(samples, SEQ, KP)
    projected_g = jnp.dot(masked_gradient, width_projection[1], preferred_element_type=f32).reshape(samples, SEQ, KP)
    first = adapter_scale * jnp.einsum(
        "stk,stq->skq", projected_x, compact_up.reshape(samples, SEQ, KQ), precision=exact)
    second = adapter_scale * jnp.einsum(
        "stk,stq->skq", projected_g, compact_down.reshape(samples, SEQ, KQ), precision=exact)
    partial_value = jnp.concatenate([first.reshape(samples, -1), second.reshape(samples, -1)], axis=1)
    features = lax.psum(partial_value, "mp")
    every_target = lax.all_gather(targets, ("dp", "mp"), axis=1, tiled=True)
    inner = jnp.dot(features, every_target.T, precision=exact)
    sample_rms = jnp.sqrt(jnp.sum(features * features, axis=1) / FEAT + epsilon)
    target_rms = jnp.sqrt(jnp.sum(every_target * every_target, axis=1) / FEAT + epsilon)
    return inner / (math.sqrt(FEAT) * sample_rms[:, None] * target_rms[None, :])


def solution(mesh):
    n_dp, n_mp = mesh.shape["dp"], mesh.shape["mp"]
    fits = n_mp == 2 and n_dp * n_mp * KQ * KQ == FEAT

    def on_device(*args):
        eight = args[0].shape[0] == 8 * SEQ
        return fused(n_dp, *args) if fits and eight else general(*args)

    in_specs = (
        P("dp", "mp"), P("dp", "mp"), P("dp"), P(None, "mp"), P("mp", None), P(None, "mp", None), P(),
        P(None, ("dp", "mp")),
    )
    return jax.shard_map(on_device, mesh=mesh, in_specs=in_specs, out_specs=P("dp", None), check_vma=False)
```

```python
import functools
import math

import jax
import jax.numpy as jnp
from jax import lax
from jax.experimental import pallas as pl
from jax.experimental.pallas import tpu as pltpu
from jax.sharding import PartitionSpec as P

SEQ = 256
KP = 256
KQ = 16
FEAT = 8192
PLANE = 4
LAG = 2

adapter_scale = 4.0
epsilon = 1e-06

f32 = jnp.float32
bf16 = jnp.bfloat16


def split(value):
    high = value.astype(bf16)
    low = (value - high.astype(f32)).astype(bf16)
    return high, low


def kernel(
    n_dp, samples,
    x_hbm, g_hbm, mask_ref, down_hbm, up_hbm, wp_hbm, rp_ref, tgt_ref, out_ref,
    xv, gv, dv, uv, wv, acol, cs, cr, ys, tp, tt, fs, fr, es, er,
    xsem, gsem, wsem, zsend, zrecv, csend, crecv, fsend, frecv, esend, erecv,
):
    me = lax.axis_index("dp")
    core = lax.axis_index("mp")
    lines = n_dp // PLANE
    group = 2 * PLANE
    mine_z = lax.div(me, PLANE)
    mine_p = lax.rem(me, PLANE)
    place = mine_p * 2 + core
    nt = tgt_ref.shape[0]
    cols = KQ * nt
    half = samples * KQ // 2

    down_copy = pltpu.make_async_copy(down_hbm, dv, wsem.at[0])
    up_copy = pltpu.make_async_copy(up_hbm, uv, wsem.at[1])
    wp_copy = pltpu.make_async_copy(wp_hbm, wv, wsem.at[2])

    def x_copy(n):
        rows = pl.ds(pl.multiple_of(n * SEQ, SEQ), SEQ)
        return pltpu.make_async_copy(x_hbm.at[rows], xv.at[n], xsem.at[n])

    def g_copy(n):
        rows = pl.ds(pl.multiple_of(n * SEQ, SEQ), SEQ)
        return pltpu.make_async_copy(g_hbm.at[rows], gv.at[n], gsem.at[n])

    down_copy.start()
    up_copy.start()
    for n in range(samples):
        x_copy(n).start()
        g_copy(n).start()
    wp_copy.start()

    def z_peer(r):
        return {"dp": lax.rem(mine_z + r, lines) * PLANE + mine_p}

    def p_peer(r):
        there = lax.rem(place + r, group)
        return {"dp": mine_z * PLANE + lax.div(there, 2), "mp": lax.rem(there, 2)}

    mesh_ids = pl.DeviceIdType.MESH
    barrier = pltpu.get_barrier_semaphore()
    for r in range(1, lines):
        pl.semaphore_signal(barrier, inc=1, device_id=z_peer(r), device_id_type=mesh_ids)
    for r in range(1, group):
        pl.semaphore_signal(barrier, inc=1, device_id=p_peer(r), device_id_type=mesh_ids)

    turned = tgt_ref[...].T
    tp[:, 0:nt] = turned
    tp[:, nt : 2 * nt] = turned
    lane = lax.broadcasted_iota(jnp.int32, (KQ, 2 * nt), 1)
    for pair in range(KQ // 2):
        even = tp[pl.ds(2 * pair, KQ, stride=KQ), :]
        odd = tp[pl.ds(2 * pair + 1, KQ, stride=KQ), :]
        tt[mine_z, :, pair * 2 * nt : (pair + 1) * 2 * nt] = jnp.where(lane < nt, even, odd)

    down_copy.wait()
    first = jnp.dot(rp_ref[1], dv[...], preferred_element_type=f32)
    high, low = split(first)
    acol[0] = jnp.concatenate([high.astype(f32), low.astype(f32)], axis=0).T.astype(bf16)
    up_copy.wait()
    second = lax.dot_general(uv[...], rp_ref[0], (((1,), (1,)), ((), ())), preferred_element_type=f32)
    high, low = split(second)
    acol[1, :, 0:KQ] = high
    acol[1, :, KQ : 2 * KQ] = low

    pl.semaphore_wait(barrier, lines - 1 + group - 1)

    def shard_copy(r):
        return pltpu.make_async_remote_copy(
            src_ref=tt.at[mine_z], dst_ref=tt.at[mine_z], send_sem=zsend.at[r], recv_sem=zrecv.at[r],
            device_id=z_peer(r), device_id_type=mesh_ids,
        )

    for r in range(1, lines):
        shard_copy(r).start()

    def c_copy(n):
        return pltpu.make_async_remote_copy(
            src_ref=cs.at[n], dst_ref=cr.at[n], send_sem=csend.at[n], recv_sem=crecv.at[n],
            device_id={"mp": 1 - core}, device_id_type=mesh_ids,
        )

    def phase_one(n):
        x_copy(n).wait()
        down = jnp.dot(xv[n], acol[0], preferred_element_type=f32)
        g_copy(n).wait()
        up = jnp.dot(gv[n], acol[1], preferred_element_type=f32)
        down_t = down.T
        up_t = up.T
        cs[n, 0:KQ] = down_t[0:KQ] + down_t[KQ : 2 * KQ]
        cs[n, KQ : 2 * KQ] = up_t[0:KQ] + up_t[KQ : 2 * KQ]
        c_copy(n).start()

    def phase_two(n):
        c_copy(n).wait_recv()
        flags = mask_ref[n].astype(f32) * adapter_scale
        total = (cs[n] + cr[n]) * flags
        high, low = split(total)
        part = lax.div(n, samples // 2)
        start = lax.rem(n, samples // 2) * KQ
        rows = pl.ds(pl.multiple_of(start, KQ), KQ)
        low_rows = pl.ds(pl.multiple_of(half + start, KQ), KQ)
        for j, (data, base) in enumerate(((xv, KQ), (gv, 0))):
            left = jnp.concatenate([high[base : base + KQ], low[base : base + KQ]], axis=0)
            out = jnp.dot(left, data[n], preferred_element_type=f32)
            y_high, y_low = split(out[0:KQ] + out[KQ : 2 * KQ])
            ys[j, part, rows] = y_high
            ys[j, part, low_rows] = y_low

    def both(n, carry):
        phase_one(n)
        phase_two(n - LAG)
        return carry

    def only_one(n, carry):
        phase_one(n)
        return carry

    def only_two(n, carry):
        phase_two(n)
        return carry

    def f_copy(h, r):
        return pltpu.make_async_remote_copy(
            src_ref=fs.at[h, lax.rem(place + r, group)], dst_ref=fr.at[h, place],
            send_sem=fsend.at[h, r], recv_sem=frecv.at[h, r],
            device_id=p_peer(r), device_id_type=mesh_ids,
        )

    quarter = half // 2
    lane_block = lax.div(lax.broadcasted_iota(jnp.int32, (quarter, 8 * KQ), 1), KQ)

    def send_features(h):
        slabs = []
        for j in range(2):
            out = jnp.dot(ys[j, h], wv[j], preferred_element_type=f32)
            out = out[0:half] + out[half : 2 * half]
            for g in range(2):
                for line in range(2):
                    slab = out[g * quarter : (g + 1) * quarter, line * 8 * KQ : (line + 1) * 8 * KQ]
                    slabs.append((g * 4 + j * 2 + line, slab))
        for e in range(group):
            piece = None
            for block, slab in slabs:
                shift = (block - e) % 8 * KQ
                moved = pltpu.roll(slab, shift, 1) if shift else slab
                piece = moved if piece is None else jnp.where(lane_block == block, moved, piece)
            fs[h, e] = piece
        for r in range(1, group):
            f_copy(h, r).start()

    cut = LAG + samples // 2
    lax.fori_loop(0, LAG, only_one, 0)
    lax.fori_loop(LAG, cut, both, 0)
    wp_copy.wait()
    send_features(0)
    lax.fori_loop(cut, samples, both, 0)
    lax.fori_loop(samples - LAG, samples, only_two, 0)
    send_features(1)

    for r in range(1, lines):
        shard_copy(r).wait()

    def fold(value):
        total = value[:, 0 : 2 * nt]
        for piece in range(1, KQ // 2):
            total = total + value[:, piece * 2 * nt : (piece + 1) * 2 * nt]
        return total

    held = tt[...].reshape(lines * KQ, cols)
    squares = fold(jnp.sum(held * held, axis=0, keepdims=True))
    squares = jnp.broadcast_to(squares, (8, 2 * nt))
    tt_high, tt_low = split(held)
    twice_high = jnp.concatenate([tt_high, tt_high], axis=0)
    twice_low = jnp.concatenate([tt_low, tt_low], axis=0)

    fr[0, place] = fs[0, place]
    fr[1, place] = fs[1, place]
    for h in range(2):
        for r in range(1, group):
            f_copy(h, r).wait()
    stacked = []
    for p in range(PLANE):
        for h in range(2):
            total = fr[h, 2 * p] + fr[h, 2 * p + 1]
            for g in range(2):
                stacked.append(jnp.where(lax.div(lane_block, 4) == g, total, 0.0))
    stacked = jnp.concatenate(stacked, axis=0)
    power = jnp.sum((stacked * stacked).reshape(PLANE * samples, KQ, 8 * KQ), axis=1)
    high, low = split(stacked)
    inner = (
        jnp.dot(high, twice_high, preferred_element_type=f32)
        + jnp.dot(low, twice_high, preferred_element_type=f32)
        + jnp.dot(high, twice_low, preferred_element_type=f32)
    )
    shape = (PLANE * samples * KQ, cols)
    row_q = lax.rem(lax.broadcasted_iota(jnp.int32, shape, 0), KQ)
    col_q = lax.div(lax.broadcasted_iota(jnp.int32, shape, 1), nt)
    inner = jnp.where(row_q == col_q, inner, 0.0)
    inner = fold(jnp.sum(inner.reshape(PLANE * samples, KQ, cols), axis=1))

    for p in range(PLANE):
        es[p, 0:8] = inner[p * samples : (p + 1) * samples]
        es[p, 8:16] = power[p * samples : (p + 1) * samples]
        es[p, 16:24] = squares

    def e_copy(r):
        return pltpu.make_async_remote_copy(
            src_ref=es.at[lax.div(lax.rem(place + r, group), 2)], dst_ref=er.at[place],
            send_sem=esend.at[r], recv_sem=erecv.at[r],
            device_id=p_peer(r), device_id_type=mesh_ids,
        )

    for r in range(1, group):
        e_copy(r).start()
    er[place] = es[mine_p]
    for n in range(samples):
        c_copy(n).wait_send()
    for r in range(1, group):
        e_copy(r).wait()
    total = jnp.sum(er[...], axis=0)
    sample_rms = jnp.sqrt(jnp.sum(total[8:16], axis=1, keepdims=True) / FEAT + epsilon)
    target_squares = total[16:24, 0:nt] + total[16:24, nt : 2 * nt]
    target_rms = jnp.sqrt(target_squares / FEAT + epsilon)
    product = total[0:8, 0:nt] + total[0:8, nt : 2 * nt]
    out_ref[...] = product / (math.sqrt(FEAT) * sample_rms * target_rms)


def fused(n_dp, inputs, cotangents, loss_token_mask, adapter_down_weight, adapter_up_weight,
          width_projection, rank_projection, targets):
    samples = inputs.shape[0] // SEQ
    width = inputs.shape[1]
    rank = adapter_down_weight.shape[0]
    nt = targets.shape[0]
    any_spec = pl.BlockSpec(memory_space=pl.ANY)
    vmem = pl.BlockSpec(memory_space=pltpu.VMEM)
    dma = pltpu.SemaphoreType.DMA
    lines = n_dp // PLANE
    group = 2 * PLANE
    return pl.pallas_call(
        functools.partial(kernel, n_dp, samples),
        out_shape=jax.ShapeDtypeStruct((samples, nt), f32),
        in_specs=[any_spec, any_spec, vmem, any_spec, any_spec, any_spec, vmem, vmem],
        out_specs=vmem,
        scratch_shapes=[
            pltpu.VMEM((samples, SEQ, width), bf16),
            pltpu.VMEM((samples, SEQ, width), bf16),
            pltpu.VMEM((rank, width), bf16),
            pltpu.VMEM((width, rank), bf16),
            pltpu.VMEM((2, width, KP), bf16),
            pltpu.VMEM((2, width, 2 * KQ), bf16),
            pltpu.VMEM((samples, 2 * KQ, SEQ), f32),
            pltpu.VMEM((samples, 2 * KQ, SEQ), f32),
            pltpu.VMEM((2, 2, samples * KQ, width), bf16),
            pltpu.VMEM((KQ * KQ, 2 * nt), f32),
            pltpu.VMEM((lines, KQ, KQ * nt), f32),
            pltpu.VMEM((2, group, samples * KQ // 4, 8 * KQ), f32),
            pltpu.VMEM((2, group, samples * KQ // 4, 8 * KQ), f32),
            pltpu.VMEM((PLANE, 24, 2 * nt), f32),
            pltpu.VMEM((group, 24, 2 * nt), f32),
            dma((samples,)), dma((samples,)), dma((3,)),
            dma((lines,)), dma((lines,)),
            dma((samples,)), dma((samples,)),
            dma((2, group)), dma((2, group)), dma((group,)), dma((group,)),
        ],
        compiler_params=pltpu.CompilerParams(
            collective_id=0, has_side_effects=True, vmem_limit_bytes=56 << 20
        ),
        name="influence",
    )(inputs, cotangents, loss_token_mask.reshape(samples, 1, SEQ), adapter_down_weight,
      adapter_up_weight, width_projection, jnp.swapaxes(rank_projection, 1, 2), targets)


def general(inputs, cotangents, loss_token_mask, adapter_down_weight, adapter_up_weight,
            width_projection, rank_projection, targets):
    samples = inputs.shape[0] // SEQ
    masked_gradient = cotangents * loss_token_mask.astype(bf16)[:, None]
    cols_first = rank_projection[0].astype(f32)
    cols_second = rank_projection[1].astype(f32)
    down_partial = jnp.dot(inputs, adapter_down_weight.T, preferred_element_type=f32)
    up_partial = jnp.dot(masked_gradient, adapter_up_weight, preferred_element_type=f32)
    exact = lax.Precision.HIGHEST
    compact_up, compact_down = lax.psum(
        (jnp.dot(up_partial, cols_first, precision=exact), jnp.dot(down_partial, cols_second, precision=exact)), "mp"
    )
    projected_x = jnp.dot(inputs, width_projection[0], preferred_element_type=f32).reshape(samples, SEQ, KP)
    projected_g = jnp.dot(masked_gradient, width_projection[1], preferred_element_type=f32).reshape(samples, SEQ, KP)
    first = adapter_scale * jnp.einsum(
        "stk,stq->skq", projected_x, compact_up.reshape(samples, SEQ, KQ), precision=exact)
    second = adapter_scale * jnp.einsum(
        "stk,stq->skq", projected_g, compact_down.reshape(samples, SEQ, KQ), precision=exact)
    partial_value = jnp.concatenate([first.reshape(samples, -1), second.reshape(samples, -1)], axis=1)
    features = lax.psum(partial_value, "mp")
    every_target = lax.all_gather(targets, ("dp", "mp"), axis=1, tiled=True)
    inner = jnp.dot(features, every_target.T, precision=exact)
    sample_rms = jnp.sqrt(jnp.sum(features * features, axis=1) / FEAT + epsilon)
    target_rms = jnp.sqrt(jnp.sum(every_target * every_target, axis=1) / FEAT + epsilon)
    return inner / (math.sqrt(FEAT) * sample_rms[:, None] * target_rms[None, :])


def solution(mesh):
    n_dp, n_mp = mesh.shape["dp"], mesh.shape["mp"]
    fits = n_mp == 2 and n_dp * n_mp * KQ * KQ == FEAT

    def on_device(*args):
        eight = args[0].shape[0] == 8 * SEQ
        return fused(n_dp, *args) if fits and eight else general(*args)

    in_specs = (
        P("dp", "mp"), P("dp", "mp"), P("dp"), P(None, "mp"), P("mp", None), P(None, "mp", None), P(),
        P(None, ("dp", "mp")),
    )
    return jax.shard_map(on_device, mesh=mesh, in_specs=in_specs, out_specs=P("dp", None), check_vma=False)
```

```python
import functools
import math

import jax
import jax.numpy as jnp
from jax import lax
from jax.experimental import pallas as pl
from jax.experimental.pallas import tpu as pltpu
from jax.sharding import PartitionSpec as P

SEQ = 256
KP = 256
KQ = 16
FEAT = 8192
PLANE = 4
LAG = 2

adapter_scale = 4.0
epsilon = 1e-06

f32 = jnp.float32
bf16 = jnp.bfloat16


def split(value):
    high = value.astype(bf16)
    low = (value - high.astype(f32)).astype(bf16)
    return high, low


def kernel(
    n_dp, samples,
    x_hbm, g_hbm, mask_ref, down_hbm, up_hbm, wp_hbm, rp_ref, tgt_ref, out_ref,
    xv, gv, dv, uv, wv, acol, cs, cr, ys, tp, tt, fs, fr, es, er, qs, qr,
    xsem, gsem, wsem, zsend, zrecv, csend, crecv, fsend, frecv, esend, erecv, qsend, qrecv,
):
    me = lax.axis_index("dp")
    core = lax.axis_index("mp")
    lines = n_dp // PLANE
    group = 2 * PLANE
    mine_z = lax.div(me, PLANE)
    mine_p = lax.rem(me, PLANE)
    place = mine_p * 2 + core
    nt = tgt_ref.shape[0]
    cols = KQ * nt
    half = samples * KQ // 2

    down_copy = pltpu.make_async_copy(down_hbm, dv, wsem.at[0])
    up_copy = pltpu.make_async_copy(up_hbm, uv, wsem.at[1])
    wp_copy = pltpu.make_async_copy(wp_hbm, wv, wsem.at[2])

    def x_copy(n):
        rows = pl.ds(pl.multiple_of(n * SEQ, SEQ), SEQ)
        return pltpu.make_async_copy(x_hbm.at[rows], xv.at[n], xsem.at[n])

    def g_copy(n):
        rows = pl.ds(pl.multiple_of(n * SEQ, SEQ), SEQ)
        return pltpu.make_async_copy(g_hbm.at[rows], gv.at[n], gsem.at[n])

    down_copy.start()
    up_copy.start()
    for n in range(samples):
        x_copy(n).start()
        g_copy(n).start()
    wp_copy.start()

    def z_peer(r):
        return {"dp": lax.rem(mine_z + r, lines) * PLANE + mine_p}

    def p_peer(r):
        there = lax.rem(place + r, group)
        return {"dp": mine_z * PLANE + lax.div(there, 2), "mp": lax.rem(there, 2)}

    mesh_ids = pl.DeviceIdType.MESH
    barrier = pltpu.get_barrier_semaphore()
    for r in range(1, lines):
        pl.semaphore_signal(barrier, inc=1, device_id=z_peer(r), device_id_type=mesh_ids)
    for r in range(1, group):
        pl.semaphore_signal(barrier, inc=1, device_id=p_peer(r), device_id_type=mesh_ids)

    turned = tgt_ref[...].T
    tp[:, 0:nt] = turned
    tp[:, nt : 2 * nt] = turned
    lane = lax.broadcasted_iota(jnp.int32, (KQ, 2 * nt), 1)
    for pair in range(KQ // 2):
        even = tp[pl.ds(2 * pair, KQ, stride=KQ), :]
        odd = tp[pl.ds(2 * pair + 1, KQ, stride=KQ), :]
        tt[mine_z, :, pair * 2 * nt : (pair + 1) * 2 * nt] = jnp.where(lane < nt, even, odd)

    down_copy.wait()
    first = jnp.dot(rp_ref[1], dv[...], preferred_element_type=f32)
    high, low = split(first)
    acol[0] = jnp.concatenate([high.astype(f32), low.astype(f32)], axis=0).T.astype(bf16)
    up_copy.wait()
    second = lax.dot_general(uv[...], rp_ref[0], (((1,), (1,)), ((), ())), preferred_element_type=f32)
    high, low = split(second)
    acol[1, :, 0:KQ] = high
    acol[1, :, KQ : 2 * KQ] = low

    pl.semaphore_wait(barrier, lines - 1 + group - 1)

    def shard_copy(r):
        return pltpu.make_async_remote_copy(
            src_ref=tt.at[mine_z], dst_ref=tt.at[mine_z], send_sem=zsend.at[r], recv_sem=zrecv.at[r],
            device_id=z_peer(r), device_id_type=mesh_ids,
        )

    for r in range(1, lines):
        shard_copy(r).start()

    def c_copy(n):
        return pltpu.make_async_remote_copy(
            src_ref=cs.at[n], dst_ref=cr.at[n], send_sem=csend.at[n], recv_sem=crecv.at[n],
            device_id={"mp": 1 - core}, device_id_type=mesh_ids,
        )

    def phase_one(n):
        x_copy(n).wait()
        down = jnp.dot(xv[n], acol[0], preferred_element_type=f32)
        g_copy(n).wait()
        up = jnp.dot(gv[n], acol[1], preferred_element_type=f32)
        down_t = down.T
        up_t = up.T
        cs[n, 0:KQ] = down_t[0:KQ] + down_t[KQ : 2 * KQ]
        cs[n, KQ : 2 * KQ] = up_t[0:KQ] + up_t[KQ : 2 * KQ]
        c_copy(n).start()

    def phase_two(n):
        c_copy(n).wait_recv()
        flags = mask_ref[n].astype(f32) * adapter_scale
        total = (cs[n] + cr[n]) * flags
        high, low = split(total)
        part = lax.div(n, samples // 2)
        start = lax.rem(n, samples // 2) * KQ
        rows = pl.ds(pl.multiple_of(start, KQ), KQ)
        low_rows = pl.ds(pl.multiple_of(half + start, KQ), KQ)
        for j, (data, base) in enumerate(((xv, KQ), (gv, 0))):
            left = jnp.concatenate([high[base : base + KQ], low[base : base + KQ]], axis=0)
            out = jnp.dot(left, data[n], preferred_element_type=f32)
            y_high, y_low = split(out[0:KQ] + out[KQ : 2 * KQ])
            ys[j, part, rows] = y_high
            ys[j, part, low_rows] = y_low

    def both(n, carry):
        phase_one(n)
        phase_two(n - LAG)
        return carry

    def only_one(n, carry):
        phase_one(n)
        return carry

    def only_two(n, carry):
        phase_two(n)
        return carry

    def f_copy(h, r):
        return pltpu.make_async_remote_copy(
            src_ref=fs.at[h, lax.rem(place + r, group)], dst_ref=fr.at[h, place],
            send_sem=fsend.at[h, r], recv_sem=frecv.at[h, r],
            device_id=p_peer(r), device_id_type=mesh_ids,
        )

    quarter = half // 2
    lane_block = lax.div(lax.broadcasted_iota(jnp.int32, (quarter, 8 * KQ), 1), KQ)

    def send_features(h):
        slabs = []
        for j in range(2):
            out = jnp.dot(ys[j, h], wv[j], preferred_element_type=f32)
            out = out[0:half] + out[half : 2 * half]
            for g in range(2):
                for line in range(2):
                    slab = out[g * quarter : (g + 1) * quarter, line * 8 * KQ : (line + 1) * 8 * KQ]
                    slabs.append((g * 4 + j * 2 + line, slab))
        for e in range(group):
            piece = None
            for block, slab in slabs:
                shift = (block - e) % 8 * KQ
                moved = pltpu.roll(slab, shift, 1) if shift else slab
                piece = moved if piece is None else jnp.where(lane_block == block, moved, piece)
            fs[h, e] = piece
        for r in range(1, group):
            f_copy(h, r).start()

    cut = LAG + samples // 2
    lax.fori_loop(0, LAG, only_one, 0)
    lax.fori_loop(LAG, cut, both, 0)
    wp_copy.wait()
    send_features(0)
    lax.fori_loop(cut, samples, both, 0)
    lax.fori_loop(samples - LAG, samples, only_two, 0)
    send_features(1)

    for r in range(1, lines):
        shard_copy(r).wait()

    def fold(value):
        total = value[:, 0 : 2 * nt]
        for piece in range(1, KQ // 2):
            total = total + value[:, piece * 2 * nt : (piece + 1) * 2 * nt]
        return total

    held = tt[...].reshape(lines * KQ, cols)
    squares = fold(jnp.sum(held * held, axis=0, keepdims=True))
    squares = jnp.broadcast_to(squares, (8, 2 * nt))
    tt_high, tt_low = split(held)
    right_side = jnp.concatenate([tt_high, tt_high, tt_low, tt_low], axis=0)
    qs[...] = squares

    def q_copy(r):
        return pltpu.make_async_remote_copy(
            src_ref=qs, dst_ref=qr.at[place], send_sem=qsend.at[r], recv_sem=qrecv.at[r],
            device_id=p_peer(r), device_id_type=mesh_ids,
        )

    for r in range(1, group):
        q_copy(r).start()
    qr[place] = squares

    few = samples // 2
    shape = (PLANE * half, cols)
    row_q = lax.rem(lax.broadcasted_iota(jnp.int32, shape, 0), KQ)
    col_q = lax.div(lax.broadcasted_iota(jnp.int32, shape, 1), nt)
    left_lane = lax.broadcasted_iota(jnp.int32, (PLANE * few, 2 * nt), 1) < nt
    for h in range(2):
        fr[h, place] = fs[h, place]
        for r in range(1, group):
            f_copy(h, r).wait()
        stacked = []
        for p in range(PLANE):
            total = fr[h, 2 * p] + fr[h, 2 * p + 1]
            for g in range(2):
                stacked.append(jnp.where(lax.div(lane_block, 4) == g, total, 0.0))
        stacked = jnp.concatenate(stacked, axis=0)
        power = jnp.sum((stacked * stacked).reshape(PLANE * few, KQ, 8 * KQ), axis=1)
        high, low = split(stacked)
        filled = (high.astype(f32) + pltpu.roll(low.astype(f32), 4 * KQ, 1)).astype(bf16)
        inner = jnp.dot(jnp.concatenate([filled, high], axis=1), right_side, preferred_element_type=f32)
        inner = jnp.where(row_q == col_q, inner, 0.0)
        inner = fold(jnp.sum(inner.reshape(PLANE * few, KQ, cols), axis=1))
        inner = inner + pltpu.roll(inner, nt, 1)
        power = power + pltpu.roll(power, nt, 1)
        message = jnp.where(left_lane, inner, power)
        for p in range(PLANE):
            es[p, h * few : (h + 1) * few] = message[p * few : (p + 1) * few]

    def e_copy(r):
        return pltpu.make_async_remote_copy(
            src_ref=es.at[lax.div(lax.rem(place + r, group), 2)], dst_ref=er.at[place],
            send_sem=esend.at[r], recv_sem=erecv.at[r],
            device_id=p_peer(r), device_id_type=mesh_ids,
        )

    for r in range(1, group):
        e_copy(r).start()
    er[place] = es[mine_p]
    for n in range(samples):
        c_copy(n).wait_send()
    for r in range(1, group):
        q_copy(r).wait()
    target_squares = jnp.sum(qr[...], axis=0)
    target_squares = target_squares[:, 0:nt] + target_squares[:, nt : 2 * nt]
    target_rms = jnp.sqrt(target_squares / FEAT + epsilon)
    for r in range(1, group):
        e_copy(r).wait()
    total = jnp.sum(er[...], axis=0)
    sample_squares = jnp.sum(total[:, nt : 2 * nt], axis=1, keepdims=True)
    sample_rms = jnp.sqrt(sample_squares / FEAT + epsilon)
    out_ref[...] = total[:, 0:nt] / (math.sqrt(FEAT) * sample_rms * target_rms)


def fused(n_dp, inputs, cotangents, loss_token_mask, adapter_down_weight, adapter_up_weight,
          width_projection, rank_projection, targets):
    samples = inputs.shape[0] // SEQ
    width = inputs.shape[1]
    rank = adapter_down_weight.shape[0]
    nt = targets.shape[0]
    any_spec = pl.BlockSpec(memory_space=pl.ANY)
    vmem = pl.BlockSpec(memory_space=pltpu.VMEM)
    dma = pltpu.SemaphoreType.DMA
    lines = n_dp // PLANE
    group = 2 * PLANE
    return pl.pallas_call(
        functools.partial(kernel, n_dp, samples),
        out_shape=jax.ShapeDtypeStruct((samples, nt), f32),
        in_specs=[any_spec, any_spec, vmem, any_spec, any_spec, any_spec, vmem, vmem],
        out_specs=vmem,
        scratch_shapes=[
            pltpu.VMEM((samples, SEQ, width), bf16),
            pltpu.VMEM((samples, SEQ, width), bf16),
            pltpu.VMEM((rank, width), bf16),
            pltpu.VMEM((width, rank), bf16),
            pltpu.VMEM((2, width, KP), bf16),
            pltpu.VMEM((2, width, 2 * KQ), bf16),
            pltpu.VMEM((samples, 2 * KQ, SEQ), f32),
            pltpu.VMEM((samples, 2 * KQ, SEQ), f32),
            pltpu.VMEM((2, 2, samples * KQ, width), bf16),
            pltpu.VMEM((KQ * KQ, 2 * nt), f32),
            pltpu.VMEM((lines, KQ, KQ * nt), f32),
            pltpu.VMEM((2, group, samples * KQ // 4, 8 * KQ), f32),
            pltpu.VMEM((2, group, samples * KQ // 4, 8 * KQ), f32),
            pltpu.VMEM((PLANE, samples, 2 * nt), f32),
            pltpu.VMEM((group, samples, 2 * nt), f32),
            pltpu.VMEM((8, 2 * nt), f32),
            pltpu.VMEM((group, 8, 2 * nt), f32),
            dma((samples,)), dma((samples,)), dma((3,)),
            dma((lines,)), dma((lines,)),
            dma((samples,)), dma((samples,)),
            dma((2, group)), dma((2, group)), dma((group,)), dma((group,)), dma((group,)), dma((group,)),
        ],
        compiler_params=pltpu.CompilerParams(
            collective_id=0, has_side_effects=True, vmem_limit_bytes=56 << 20
        ),
        name="influence",
    )(inputs, cotangents, loss_token_mask.reshape(samples, 1, SEQ), adapter_down_weight,
      adapter_up_weight, width_projection, jnp.swapaxes(rank_projection, 1, 2), targets)


def general(inputs, cotangents, loss_token_mask, adapter_down_weight, adapter_up_weight,
            width_projection, rank_projection, targets):
    samples = inputs.shape[0] // SEQ
    masked_gradient = cotangents * loss_token_mask.astype(bf16)[:, None]
    cols_first = rank_projection[0].astype(f32)
    cols_second = rank_projection[1].astype(f32)
    down_partial = jnp.dot(inputs, adapter_down_weight.T, preferred_element_type=f32)
    up_partial = jnp.dot(masked_gradient, adapter_up_weight, preferred_element_type=f32)
    exact = lax.Precision.HIGHEST
    compact_up, compact_down = lax.psum(
        (jnp.dot(up_partial, cols_first, precision=exact), jnp.dot(down_partial, cols_second, precision=exact)), "mp"
    )
    projected_x = jnp.dot(inputs, width_projection[0], preferred_element_type=f32).reshape(samples, SEQ, KP)
    projected_g = jnp.dot(masked_gradient, width_projection[1], preferred_element_type=f32).reshape(samples, SEQ, KP)
    first = adapter_scale * jnp.einsum(
        "stk,stq->skq", projected_x, compact_up.reshape(samples, SEQ, KQ), precision=exact)
    second = adapter_scale * jnp.einsum(
        "stk,stq->skq", projected_g, compact_down.reshape(samples, SEQ, KQ), precision=exact)
    partial_value = jnp.concatenate([first.reshape(samples, -1), second.reshape(samples, -1)], axis=1)
    features = lax.psum(partial_value, "mp")
    every_target = lax.all_gather(targets, ("dp", "mp"), axis=1, tiled=True)
    inner = jnp.dot(features, every_target.T, precision=exact)
    sample_rms = jnp.sqrt(jnp.sum(features * features, axis=1) / FEAT + epsilon)
    target_rms = jnp.sqrt(jnp.sum(every_target * every_target, axis=1) / FEAT + epsilon)
    return inner / (math.sqrt(FEAT) * sample_rms[:, None] * target_rms[None, :])


def solution(mesh):
    n_dp, n_mp = mesh.shape["dp"], mesh.shape["mp"]
    fits = n_mp == 2 and n_dp * n_mp * KQ * KQ == FEAT

    def on_device(*args):
        eight = args[0].shape[0] == 8 * SEQ
        return fused(n_dp, *args) if fits and eight else general(*args)

    in_specs = (
        P("dp", "mp"), P("dp", "mp"), P("dp"), P(None, "mp"), P("mp", None), P(None, "mp", None), P(),
        P(None, ("dp", "mp")),
    )
    return jax.shard_map(on_device, mesh=mesh, in_specs=in_specs, out_specs=P("dp", None), check_vma=False)
```

```python
import functools
import math

import jax
import jax.numpy as jnp
from jax import lax
from jax.experimental import pallas as pl
from jax.experimental.pallas import tpu as pltpu
from jax.sharding import PartitionSpec as P

SEQ = 256
KP = 256
KQ = 16
FEAT = 8192
PLANE = 4
LAG = 2

adapter_scale = 4.0
epsilon = 1e-06

f32 = jnp.float32
bf16 = jnp.bfloat16


def split(value):
    high = value.astype(bf16)
    low = (value - high.astype(f32)).astype(bf16)
    return high, low


def kernel(
    n_dp, samples,
    x_hbm, g_hbm, mask_ref, down_hbm, up_hbm, wp_hbm, rp_ref, tgt_ref, out_ref,
    xv, gv, dv, uv, wv, acol, cs, cr, ys, tp, tt, fs, fr, es, er, qs, qr,
    xsem, gsem, wsem, zsend, zrecv, csend, crecv, fsend, frecv, esend, erecv, qsend, qrecv,
):
    me = lax.axis_index("dp")
    core = lax.axis_index("mp")
    lines = n_dp // PLANE
    group = 2 * PLANE
    mine_z = lax.div(me, PLANE)
    mine_p = lax.rem(me, PLANE)
    place = mine_p * 2 + core
    nt = tgt_ref.shape[0]
    cols = KQ * nt
    half = samples * KQ // 2

    down_copy = pltpu.make_async_copy(down_hbm, dv, wsem.at[0])
    up_copy = pltpu.make_async_copy(up_hbm, uv, wsem.at[1])
    wp_copy = pltpu.make_async_copy(wp_hbm, wv, wsem.at[2])

    def x_copy(n):
        rows = pl.ds(pl.multiple_of(n * SEQ, SEQ), SEQ)
        return pltpu.make_async_copy(x_hbm.at[rows], xv.at[n], xsem.at[n])

    def g_copy(n):
        rows = pl.ds(pl.multiple_of(n * SEQ, SEQ), SEQ)
        return pltpu.make_async_copy(g_hbm.at[rows], gv.at[n], gsem.at[n])

    down_copy.start()
    up_copy.start()
    for n in range(samples):
        x_copy(n).start()
        g_copy(n).start()
    wp_copy.start()

    def z_peer(r):
        return {"dp": lax.rem(mine_z + r, lines) * PLANE + mine_p}

    def p_peer(r):
        there = lax.rem(place + r, group)
        return {"dp": mine_z * PLANE + lax.div(there, 2), "mp": lax.rem(there, 2)}

    mesh_ids = pl.DeviceIdType.MESH
    barrier = pltpu.get_barrier_semaphore()
    for r in range(1, lines):
        pl.semaphore_signal(barrier, inc=1, device_id=z_peer(r), device_id_type=mesh_ids)
    for r in range(1, group):
        pl.semaphore_signal(barrier, inc=1, device_id=p_peer(r), device_id_type=mesh_ids)

    turned = tgt_ref[...].T
    tp[:, 0:nt] = turned
    tp[:, nt : 2 * nt] = turned
    lane = lax.broadcasted_iota(jnp.int32, (KQ, 2 * nt), 1)
    for pair in range(KQ // 2):
        even = tp[pl.ds(2 * pair, KQ, stride=KQ), :]
        odd = tp[pl.ds(2 * pair + 1, KQ, stride=KQ), :]
        tt[mine_z, :, pair * 2 * nt : (pair + 1) * 2 * nt] = jnp.where(lane < nt, even, odd)

    down_copy.wait()
    first = jnp.dot(rp_ref[1], dv[...], preferred_element_type=f32)
    high, low = split(first)
    acol[0] = jnp.concatenate([high, low], axis=0)
    up_copy.wait()
    second = lax.dot_general(rp_ref[0], uv[...], (((1,), (1,)), ((), ())), preferred_element_type=f32)
    high, low = split(second)
    acol[1] = jnp.concatenate([high, low], axis=0)

    pl.semaphore_wait(barrier, lines - 1 + group - 1)

    def shard_copy(r):
        return pltpu.make_async_remote_copy(
            src_ref=tt.at[mine_z], dst_ref=tt.at[mine_z], send_sem=zsend.at[r], recv_sem=zrecv.at[r],
            device_id=z_peer(r), device_id_type=mesh_ids,
        )

    for r in range(1, lines):
        shard_copy(r).start()

    def c_copy(n):
        return pltpu.make_async_remote_copy(
            src_ref=cs.at[n], dst_ref=cr.at[n], send_sem=csend.at[n], recv_sem=crecv.at[n],
            device_id={"mp": 1 - core}, device_id_type=mesh_ids,
        )

    def phase_one(n):
        down_t = lax.dot_general(acol[0], xv[n], (((1,), (1,)), ((), ())), preferred_element_type=f32)
        up_t = lax.dot_general(acol[1], gv[n], (((1,), (1,)), ((), ())), preferred_element_type=f32)
        cs[n, 0:KQ] = down_t[0:KQ] + down_t[KQ : 2 * KQ]
        cs[n, KQ : 2 * KQ] = up_t[0:KQ] + up_t[KQ : 2 * KQ]

    def phase_two(n):
        flags = mask_ref[n].astype(f32) * adapter_scale
        total = (cs[n] + cr[n]) * flags
        high, low = split(total)
        part = lax.div(n, samples // 2)
        start = lax.rem(n, samples // 2) * KQ
        rows = pl.ds(pl.multiple_of(start, KQ), KQ)
        low_rows = pl.ds(pl.multiple_of(half + start, KQ), KQ)
        for j, (data, base) in enumerate(((xv, KQ), (gv, 0))):
            left = jnp.concatenate([high[base : base + KQ], low[base : base + KQ]], axis=0)
            out = jnp.dot(left, data[n], preferred_element_type=f32)
            y_high, y_low = split(out[0:KQ] + out[KQ : 2 * KQ])
            ys[j, part, rows] = y_high
            ys[j, part, low_rows] = y_low

    def both(n, carry):
        x_copy(n).wait()
        g_copy(n).wait()
        c_copy(n - LAG).wait_recv()
        phase_one(n)
        phase_two(n - LAG)
        c_copy(n).start()
        return carry

    def only_one(n, carry):
        x_copy(n).wait()
        g_copy(n).wait()
        phase_one(n)
        c_copy(n).start()
        return carry

    def only_two(n, carry):
        c_copy(n).wait_recv()
        phase_two(n)
        return carry

    def f_copy(h, r):
        return pltpu.make_async_remote_copy(
            src_ref=fs.at[h, lax.rem(place + r, group)], dst_ref=fr.at[h, place],
            send_sem=fsend.at[h, r], recv_sem=frecv.at[h, r],
            device_id=p_peer(r), device_id_type=mesh_ids,
        )

    quarter = half // 2
    lane_block = lax.div(lax.broadcasted_iota(jnp.int32, (quarter, 8 * KQ), 1), KQ)

    def send_features(h):
        slabs = []
        for j in range(2):
            out = jnp.dot(ys[j, h], wv[j], preferred_element_type=f32)
            out = out[0:half] + out[half : 2 * half]
            for g in range(2):
                for line in range(2):
                    slab = out[g * quarter : (g + 1) * quarter, line * 8 * KQ : (line + 1) * 8 * KQ]
                    slabs.append((g * 4 + j * 2 + line, slab))
        for e in range(group):
            piece = None
            for block, slab in slabs:
                shift = (block - e) % 8 * KQ
                moved = pltpu.roll(slab, shift, 1) if shift else slab
                piece = moved if piece is None else jnp.where(lane_block == block, moved, piece)
            fs[h, e] = piece
        for r in range(1, group):
            f_copy(h, r).start()

    cut = LAG + samples // 2
    lax.fori_loop(0, LAG, only_one, 0)
    lax.fori_loop(LAG, cut, both, 0)
    wp_copy.wait()
    send_features(0)
    lax.fori_loop(cut, samples, both, 0)
    lax.fori_loop(samples - LAG, samples, only_two, 0)
    send_features(1)

    for r in range(1, lines):
        shard_copy(r).wait()

    def fold(value):
        total = value[:, 0 : 2 * nt]
        for piece in range(1, KQ // 2):
            total = total + value[:, piece * 2 * nt : (piece + 1) * 2 * nt]
        return total

    held = tt[...].reshape(lines * KQ, cols)
    squares = fold(jnp.sum(held * held, axis=0, keepdims=True))
    squares = jnp.broadcast_to(squares, (8, 2 * nt))
    tt_high, tt_low = split(held)
    right_side = jnp.concatenate([tt_high, tt_high, tt_low, tt_low], axis=0)
    qs[...] = squares

    def q_copy(r):
        return pltpu.make_async_remote_copy(
            src_ref=qs, dst_ref=qr.at[place], send_sem=qsend.at[r], recv_sem=qrecv.at[r],
            device_id=p_peer(r), device_id_type=mesh_ids,
        )

    for r in range(1, group):
        q_copy(r).start()
    qr[place] = squares

    few = samples // 2
    shape = (PLANE * half, cols)
    row_q = lax.rem(lax.broadcasted_iota(jnp.int32, shape, 0), KQ)
    col_q = lax.div(lax.broadcasted_iota(jnp.int32, shape, 1), nt)
    left_lane = lax.broadcasted_iota(jnp.int32, (PLANE * few, 2 * nt), 1) < nt
    for h in range(2):
        fr[h, place] = fs[h, place]
        for r in range(1, group):
            f_copy(h, r).wait()
        stacked = []
        for p in range(PLANE):
            total = fr[h, 2 * p] + fr[h, 2 * p + 1]
            for g in range(2):
                stacked.append(jnp.where(lax.div(lane_block, 4) == g, total, 0.0))
        stacked = jnp.concatenate(stacked, axis=0)
        power = jnp.sum((stacked * stacked).reshape(PLANE * few, KQ, 8 * KQ), axis=1)
        high, low = split(stacked)
        filled = (high.astype(f32) + pltpu.roll(low.astype(f32), 4 * KQ, 1)).astype(bf16)
        inner = jnp.dot(jnp.concatenate([filled, high], axis=1), right_side, preferred_element_type=f32)
        inner = jnp.where(row_q == col_q, inner, 0.0)
        inner = fold(jnp.sum(inner.reshape(PLANE * few, KQ, cols), axis=1))
        inner = inner + pltpu.roll(inner, nt, 1)
        power = power + pltpu.roll(power, nt, 1)
        message = jnp.where(left_lane, inner, power)
        for p in range(PLANE):
            es[p, h * few : (h + 1) * few] = message[p * few : (p + 1) * few]

    def e_copy(r):
        return pltpu.make_async_remote_copy(
            src_ref=es.at[lax.div(lax.rem(place + r, group), 2)], dst_ref=er.at[place],
            send_sem=esend.at[r], recv_sem=erecv.at[r],
            device_id=p_peer(r), device_id_type=mesh_ids,
        )

    for r in range(1, group):
        e_copy(r).start()
    er[place] = es[mine_p]
    for n in range(samples):
        c_copy(n).wait_send()
    for r in range(1, group):
        q_copy(r).wait()
    target_squares = jnp.sum(qr[...], axis=0)
    target_squares = target_squares[:, 0:nt] + target_squares[:, nt : 2 * nt]
    target_rms = jnp.sqrt(target_squares / FEAT + epsilon)
    for r in range(1, group):
        e_copy(r).wait()
    total = jnp.sum(er[...], axis=0)
    sample_squares = jnp.sum(total[:, nt : 2 * nt], axis=1, keepdims=True)
    sample_rms = jnp.sqrt(sample_squares / FEAT + epsilon)
    out_ref[...] = total[:, 0:nt] / (math.sqrt(FEAT) * sample_rms * target_rms)


def fused(n_dp, inputs, cotangents, loss_token_mask, adapter_down_weight, adapter_up_weight,
          width_projection, rank_projection, targets):
    samples = inputs.shape[0] // SEQ
    width = inputs.shape[1]
    rank = adapter_down_weight.shape[0]
    nt = targets.shape[0]
    any_spec = pl.BlockSpec(memory_space=pl.ANY)
    vmem = pl.BlockSpec(memory_space=pltpu.VMEM)
    dma = pltpu.SemaphoreType.DMA
    lines = n_dp // PLANE
    group = 2 * PLANE
    return pl.pallas_call(
        functools.partial(kernel, n_dp, samples),
        out_shape=jax.ShapeDtypeStruct((samples, nt), f32),
        in_specs=[any_spec, any_spec, vmem, any_spec, any_spec, any_spec, vmem, vmem],
        out_specs=vmem,
        scratch_shapes=[
            pltpu.VMEM((samples, SEQ, width), bf16),
            pltpu.VMEM((samples, SEQ, width), bf16),
            pltpu.VMEM((rank, width), bf16),
            pltpu.VMEM((width, rank), bf16),
            pltpu.VMEM((2, width, KP), bf16),
            pltpu.VMEM((2, 2 * KQ, width), bf16),
            pltpu.VMEM((samples, 2 * KQ, SEQ), f32),
            pltpu.VMEM((samples, 2 * KQ, SEQ), f32),
            pltpu.VMEM((2, 2, samples * KQ, width), bf16),
            pltpu.VMEM((KQ * KQ, 2 * nt), f32),
            pltpu.VMEM((lines, KQ, KQ * nt), f32),
            pltpu.VMEM((2, group, samples * KQ // 4, 8 * KQ), f32),
            pltpu.VMEM((2, group, samples * KQ // 4, 8 * KQ), f32),
            pltpu.VMEM((PLANE, samples, 2 * nt), f32),
            pltpu.VMEM((group, samples, 2 * nt), f32),
            pltpu.VMEM((8, 2 * nt), f32),
            pltpu.VMEM((group, 8, 2 * nt), f32),
            dma((samples,)), dma((samples,)), dma((3,)),
            dma((lines,)), dma((lines,)),
            dma((samples,)), dma((samples,)),
            dma((2, group)), dma((2, group)), dma((group,)), dma((group,)), dma((group,)), dma((group,)),
        ],
        compiler_params=pltpu.CompilerParams(
            collective_id=0, has_side_effects=True, vmem_limit_bytes=56 << 20
        ),
        name="influence",
    )(inputs, cotangents, loss_token_mask.reshape(samples, 1, SEQ), adapter_down_weight,
      adapter_up_weight, width_projection, jnp.swapaxes(rank_projection, 1, 2), targets)


def general(inputs, cotangents, loss_token_mask, adapter_down_weight, adapter_up_weight,
            width_projection, rank_projection, targets):
    samples = inputs.shape[0] // SEQ
    masked_gradient = cotangents * loss_token_mask.astype(bf16)[:, None]
    cols_first = rank_projection[0].astype(f32)
    cols_second = rank_projection[1].astype(f32)
    down_partial = jnp.dot(inputs, adapter_down_weight.T, preferred_element_type=f32)
    up_partial = jnp.dot(masked_gradient, adapter_up_weight, preferred_element_type=f32)
    exact = lax.Precision.HIGHEST
    compact_up, compact_down = lax.psum(
        (jnp.dot(up_partial, cols_first, precision=exact), jnp.dot(down_partial, cols_second, precision=exact)), "mp"
    )
    projected_x = jnp.dot(inputs, width_projection[0], preferred_element_type=f32).reshape(samples, SEQ, KP)
    projected_g = jnp.dot(masked_gradient, width_projection[1], preferred_element_type=f32).reshape(samples, SEQ, KP)
    first = adapter_scale * jnp.einsum(
        "stk,stq->skq", projected_x, compact_up.reshape(samples, SEQ, KQ), precision=exact)
    second = adapter_scale * jnp.einsum(
        "stk,stq->skq", projected_g, compact_down.reshape(samples, SEQ, KQ), precision=exact)
    partial_value = jnp.concatenate([first.reshape(samples, -1), second.reshape(samples, -1)], axis=1)
    features = lax.psum(partial_value, "mp")
    every_target = lax.all_gather(targets, ("dp", "mp"), axis=1, tiled=True)
    inner = jnp.dot(features, every_target.T, precision=exact)
    sample_rms = jnp.sqrt(jnp.sum(features * features, axis=1) / FEAT + epsilon)
    target_rms = jnp.sqrt(jnp.sum(every_target * every_target, axis=1) / FEAT + epsilon)
    return inner / (math.sqrt(FEAT) * sample_rms[:, None] * target_rms[None, :])


def solution(mesh):
    n_dp, n_mp = mesh.shape["dp"], mesh.shape["mp"]
    fits = n_mp == 2 and n_dp * n_mp * KQ * KQ == FEAT

    def on_device(*args):
        eight = args[0].shape[0] == 8 * SEQ
        return fused(n_dp, *args) if fits and eight else general(*args)

    in_specs = (
        P("dp", "mp"), P("dp", "mp"), P("dp"), P(None, "mp"), P("mp", None), P(None, "mp", None), P(),
        P(None, ("dp", "mp")),
    )
    return jax.shard_map(on_device, mesh=mesh, in_specs=in_specs, out_specs=P("dp", None), check_vma=False)
```
